32 devices in a mesh: wide: 16 (over z, y, core), narrow: 2 (over x).
Axes of the slice: x: 2, y: 2, z: 4, core: 2. Of those that a mesh axis runs over, the one named last changes fastest.
Arguments:
- block_input: float32 [32, 2, 256, 1152], P(('wide', 'narrow')), may hold values from -6 to 6
- text: float32 [32, 120, 1152], P(('wide', 'narrow')), may hold values from -6 to 6
- modulation: float32 [32, 6, 1152], P(('wide', 'narrow')), may hold values from -2 to 2
- text_lengths: int32 [32], P(('wide', 'narrow')), may hold values from 1 to 120, as said below
- bucket: int32 [32], P(('wide', 'narrow')), may hold values from 0 to 1
- frames: int32 [32], P(('wide', 'narrow')), may hold values from 1 to 2
- cotangent: float32 [32, 2, 256, 1152], P(('wide', 'narrow')), may hold values from -6 to 6
- spatialqkv: float32 [1152, 3456], P('narrow', 'wide'), may hold values from -0.1875 to 0.1875
- spatialout: float32 [1152, 1152], P('narrow', 'wide'), may hold values from -0.75 to 0.75
- temporalqkv: float32 [1152, 3456], P('narrow', 'wide'), may hold values from -0.1875 to 0.1875
- temporalout: float32 [1152, 1152], P('narrow', 'wide'), may hold values from -0.1875 to 0.1875
- crossquery: float32 [1152, 1152], P('narrow', 'wide'), may hold values from -0.1875 to 0.1875
- crosskeyval: float32 [1152, 2304], P('narrow', 'wide'), may hold values from -0.1875 to 0.1875
- crossout: float32 [1152, 1152], P('narrow', 'wide'), may hold values from -0.375 to 0.375
- feedup: float32 [1152, 4608], P('narrow', 'wide'), may hold values from -0.1875 to 0.1875
- feeddown: float32 [4608, 1152], P('narrow', 'wide'), may hold values from -0.125 to 0.125
- vectors: float32 [16, 1152], P('narrow', 'wide'), may hold values from -2 to 2
- feedbias: float32 [4608], P(('wide', 'narrow')), may hold values from -2 to 2
Outputs:
- block_output: float32 [32, 2, 256, 1152], P(('wide', 'narrow'))
- input_grad: float32 [32, 2, 256, 1152], P(('wide', 'narrow'))
- text_grad: float32 [32, 120, 1152], P(('wide', 'narrow'))
- spatialqkv_grad: float32 [1152, 3456], P('narrow', 'wide')
- spatialout_grad: float32 [1152, 1152], P('narrow', 'wide')
- temporalqkv_grad: float32 [1152, 3456], P('narrow', 'wide')
- temporalout_grad: float32 [1152, 1152], P('narrow', 'wide')
- crossquery_grad: float32 [1152, 1152], P('narrow', 'wide')
- crosskeyval_grad: float32 [1152, 2304], P('narrow', 'wide')
- crossout_grad: float32 [1152, 1152], P('narrow', 'wide')
- feedup_grad: float32 [1152, 4608], P('narrow', 'wide')
- feeddown_grad: float32 [4608, 1152], P('narrow', 'wide')
- vectors_grad: float32 [16, 1152], P('narrow', 'wide')
- feedbias_grad: float32 [4608], P(('wide', 'narrow'))
The draws below stay inside these ranges and needn't reach their ends.
Inputs may be any that keep to these rules, and one draw needn't show every extreme that they name: `text_lengths`: some sample uses all 120 text tokens. `frames`: read only where bucket is 0.
All inputs are finite; a program needn't handle non-finite values.
Results may differ from the reference program's by a relative error of at most 0.039.
Values may be sent and summed in bfloat16 or wider, within the bound.
A program may use at most 320 MiB of HBM per device.

```python
import math
from functools import partial
import jax
import jax.numpy as jnp
from jax import lax

D = 1152
HEADS = 16
HEAD = 72
FF = 4608
TXT = 120
PATCH = 256
FRAMES = 2
SAMPLES = 32


def draw_text_lengths(key, part):
    lengths = jax.random.randint(key, (SAMPLES,), 1, TXT + 1, dtype=jnp.int32)
    chosen = jax.random.randint(jax.random.fold_in(key, 11), (), 0, SAMPLES, dtype=jnp.int32)
    return jnp.where(jnp.arange(SAMPLES, dtype=jnp.int32) == chosen, jnp.int32(TXT), lengths).astype(jnp.int32)


def with_ends(drawn, key, low, largest):
    spot = [jax.random.randint(jax.random.fold_in(key, axis), (), 0, length) for axis, length in enumerate(drawn.shape)]
    widest = drawn.shape.index(max(drawn.shape))
    neighbour = spot[:widest] + [(spot[widest] + 1) % drawn.shape[widest]] + spot[widest + 1:]
    return drawn.at[tuple(spot)].set(low).at[tuple(neighbour)].set(largest)


def block_scale(key, shape, cuts, least, largest):
    factor_of = 1.0
    for position, blocks in cuts:
        steps = jax.random.uniform(jax.random.fold_in(jax.random.fold_in(key, 6), position), (blocks,), jnp.float32, least / len(cuts), largest / len(cuts))
        factor_of = factor_of * jnp.repeat(jnp.exp(steps), shape[position] // blocks).reshape((-1,) + (1,) * (len(shape) - 1 - position))
    return factor_of


def centred(rng, dims, scale, bound, cuts=(), held_as=jnp.bfloat16):
    array = jax.random.normal(rng, dims, jnp.float32) * scale
    if len(cuts) > 0:
        array = block_scale(rng, dims, cuts, -0.22, 0.18) * array
    return jnp.clip(array, min=-bound, max=bound).astype(held_as)


def setup_inputs(seed: int = 0) -> dict:
    arg_keys = jax.random.split(jax.random.key(seed), 19)
    return {
        "block_input": centred(arg_keys[0], (SAMPLES, FRAMES, PATCH, D), 1.0, 6.0, ((0, 32),), jnp.float32),
        "text": centred(arg_keys[1], (SAMPLES, TXT, D), 1.0, 6.0, ((0, 32),), jnp.float32),
        "modulation": centred(arg_keys[2], (SAMPLES, 6, D), 0.3, 2.0, ((0, 32),), jnp.float32),
        "text_lengths": draw_text_lengths(jax.random.fold_in(arg_keys[18], 71), 0),
        "bucket": with_ends(jax.random.randint(arg_keys[4], (SAMPLES,), 0, 2), jax.random.fold_in(arg_keys[4], 1), 0, 1).astype(jnp.int32),
        "frames": with_ends(jax.random.randint(arg_keys[5], (SAMPLES,), 1, 3), jax.random.fold_in(arg_keys[5], 1), 1, 2).astype(jnp.int32),
        "cotangent": centred(arg_keys[6], (SAMPLES, FRAMES, PATCH, D), 1.0, 6.0, ((0, 32),), jnp.float32),
        "spatialqkv": centred(arg_keys[7], (D, 3 * D), D ** -0.5, 0.1875, ((0, 2), (1, 16)), jnp.float32),
        "spatialout": centred(arg_keys[8], (D, D), (D // 16) ** -0.5, 0.75, ((0, 2), (1, 16)), jnp.float32),
        "temporalqkv": centred(arg_keys[9], (D, 3 * D), D ** -0.5, 0.1875, ((0, 2), (1, 16)), jnp.float32),
        "temporalout": centred(arg_keys[10], (D, D), D ** -0.5, 0.1875, ((0, 2), (1, 16)), jnp.float32),
        "crossquery": centred(arg_keys[11], (D, D), D ** -0.5, 0.1875, ((0, 2), (1, 16)), jnp.float32),
        "crosskeyval": centred(arg_keys[12], (D, 2 * D), D ** -0.5, 0.1875, ((0, 2), (1, 16)), jnp.float32),
        "crossout": centred(arg_keys[13], (D, D), (D // 4) ** -0.5, 0.375, ((0, 2), (1, 16)), jnp.float32),
        "feedup": centred(arg_keys[14], (D, FF), D ** -0.5, 0.1875, ((0, 2), (1, 16)), jnp.float32),
        "feeddown": centred(arg_keys[15], (FF, D), (FF // 2) ** -0.5, 0.125, ((0, 2), (1, 16)), jnp.float32),
        "vectors": centred(arg_keys[16], (16, D), 0.3, 2.0, ((0, 2), (1, 16)), jnp.float32),
        "feedbias": centred(arg_keys[17], (FF,), 0.3, 2.0, ((0, 32),), jnp.float32),
    }


@jax.custom_vjp
def low(v):
    return lax.optimization_barrier(v.astype(jnp.bfloat16)).astype(jnp.float32)

@jax.custom_vjp
def low_back(v):
    return v

def low_keep(v):
    return (low(v), None)

def low_pass(kept, grad):
    return (grad,)

def back_keep(v):
    return (v, None)

def back_low(kept, grad):
    return (low(grad),)
low.defvjp(low_keep, low_pass)
low_back.defvjp(back_keep, back_low)

def matmul(left, right):
    return jnp.dot(left, right, precision=lax.Precision.HIGHEST)

def rounded_both(value):
    return low_back(low(value))

def layer_norm(value):
    mean = lax.optimization_barrier(jnp.mean(value, axis=-1, keepdims=True))
    centered = value - mean
    variance = lax.optimization_barrier(jnp.mean(centered * centered, axis=-1, keepdims=True))
    return centered * lax.rsqrt(variance + 1e-06)

def softmax_rows(scores):
    top = lax.optimization_barrier(jnp.max(scores, axis=-1, keepdims=True))
    powers = jnp.exp(scores - top)
    return powers / lax.optimization_barrier(jnp.sum(powers, axis=-1, keepdims=True))

def masked(allowed, scores):
    return jnp.where(allowed, scores, jnp.full(scores.shape, -1000000000.0, scores.dtype))

def temporal_mix(projected, pair):
    width = HEADS * HEAD
    split = [projected[:, index * width:(index + 1) * width].reshape(FRAMES, -1, HEADS, HEAD) for index in range(3)]
    scores = jnp.einsum('rphe,sphe->phrs', split[0], split[1], precision=lax.Precision.HIGHEST) * HEAD ** (-0.5)
    scores = masked(pair, scores)
    mixed = jnp.einsum('phrs,sphe->rphe', softmax_rows(scores), split[2], precision=lax.Precision.HIGHEST)
    return mixed.reshape(-1, width)

def attend(queries, keys, values, allowed):
    scores = low_back(jnp.einsum('lhe,mhe->hlm', queries, keys, precision=lax.Precision.HIGHEST) * HEAD ** (-0.5))
    scores = masked(allowed[None], scores)
    probs = low(softmax_rows(scores))
    return rounded_both(jnp.einsum('hlm,mhe->lhe', probs, values, precision=lax.Precision.HIGHEST))

def clip_forward(weights, block, words, table_in, length, kind, count):
    spatial_in, spatial_out, temporal_in, temporal_out, cross_query, cross_keyval, cross_out, feed_up, feed_down, vectors, feed_bias = weights
    tokens = FRAMES * PATCH
    width = HEADS * HEAD
    blank = jnp.zeros((width,), jnp.float32).astype(vectors.dtype)
    table = vectors[0:6] + table_in
    flat = block.reshape(tokens, width)
    entered = low(layer_norm(flat) * (1.0 + table[1]) + table[0])
    projected = matmul(entered, spatial_in) + jnp.concatenate([vectors[6], blank, vectors[7]])
    queries = rounded_both(projected[:, :width]).reshape(tokens, HEADS, HEAD)
    keys = rounded_both(projected[:, width:2 * width]).reshape(tokens, HEADS, HEAD)
    values = rounded_both(projected[:, 2 * width:]).reshape(tokens, HEADS, HEAD)
    index = jnp.arange(tokens, dtype=jnp.int32)
    segment = jnp.where(kind.astype(jnp.int32) == 0, index // PATCH, jnp.zeros((tokens,), jnp.int32)).astype(jnp.int32)
    allowed = segment[:, None] == segment[None, :]
    attended = attend(queries, keys, values, allowed).reshape(tokens, width)
    spatial = low_back(matmul(attended, spatial_out) + vectors[8])
    first = flat + table[2] * spatial
    temporal_proj = low_back(matmul(low(first), temporal_in) + jnp.concatenate([vectors[9], blank, vectors[10]]))
    pair = jnp.eye(FRAMES, dtype=bool) | (kind.astype(jnp.int32) == 0) & (count.astype(jnp.int32) == 2)
    temporal_att = rounded_both(temporal_mix(temporal_proj, pair))
    temporal = low_back(matmul(temporal_att, temporal_out) + vectors[11])
    second = first + table[2] * temporal
    query_text = rounded_both(matmul(low(second), cross_query) + vectors[12]).reshape(tokens, HEADS, HEAD)
    keyval = matmul(low(words), cross_keyval) + jnp.concatenate([blank, vectors[13]])
    key_text = rounded_both(keyval[:, :width]).reshape(-1, HEADS, HEAD)
    value_text = rounded_both(keyval[:, width:]).reshape(-1, HEADS, HEAD)
    text_mask = (jnp.arange(words.shape[0], dtype=jnp.int32) < length.astype(jnp.int32))[None, :]
    cross_att = attend(query_text, key_text, value_text, text_mask).reshape(tokens, width)
    third = second + low_back(matmul(cross_att, cross_out) + vectors[14])
    normed = low(layer_norm(third) * (1.0 + table[4]) + table[3])
    hidden = low_back(matmul(normed, feed_up) + feed_bias)
    activated = low(jax.nn.gelu(hidden, approximate=True))
    feed = low_back(matmul(activated, feed_down) + vectors[15])
    return (third + table[5] * feed).reshape(FRAMES, PATCH, width)

def reference(block_input, text, modulation, text_lengths, bucket, frames, cotangent, spatialqkv, spatialout, temporalqkv, temporalout, crossquery, crosskeyval, crossout, feedup, feeddown, vectors, feedbias):
    group = math.gcd(8, SAMPLES)
    masters = tuple((piece.astype(jnp.float32) for piece in (spatialqkv, spatialout, temporalqkv, temporalout, crossquery, crosskeyval, crossout, feedup, feeddown, vectors, feedbias)))
    block_in = block_input.astype(jnp.float32)
    text_in = text.astype(jnp.float32)
    table_all = modulation.astype(jnp.float32)
    lengths = text_lengths.astype(jnp.int32)
    kinds = bucket.astype(jnp.int32)
    counts = frames.astype(jnp.int32)

    def forward(params, inputs, texts):
        rounded = tuple((low(piece) for piece in params))

        def run_group(items):
            return jax.vmap(partial(clip_forward, rounded))(items[0], items[1], items[2], items[3], items[4], items[5])
        stacked = tuple((piece.reshape((SAMPLES // group, group) + piece.shape[1:]) for piece in (inputs, texts, table_all, lengths, kinds, counts)))
        result = lax.map(jax.checkpoint(run_group), stacked)
        return result.reshape(inputs.shape)
    output, pullback = jax.vjp(forward, masters, block_in, text_in)
    grads, input_grad, text_grad = pullback(cotangent.astype(jnp.float32).astype(output.dtype))
    return (output, input_grad, text_grad, grads[0], grads[1], grads[2], grads[3], grads[4], grads[5], grads[6], grads[7], grads[8], grads[9], grads[10])
```

```python
from functools import partial

import jax
import jax.numpy as jnp
from jax import lax
from jax.experimental import pallas as pl
from jax.experimental.pallas import tpu as pltpu
from jax.sharding import PartitionSpec as P

HEADS = 16
HEAD = 72
PATCH = 256
FRAMES = 2


def layer_norm(value):
    mean = jnp.mean(value, axis=-1, keepdims=True)
    centered = value - mean
    variance = jnp.mean(centered * centered, axis=-1, keepdims=True)
    return centered * lax.rsqrt(variance + 1e-06)


def modulate(value, shift, scale):
    return layer_norm(value) * (1.0 + scale) + shift


def softmax_rows(scores):
    top = jnp.max(scores, axis=-1, keepdims=True)
    powers = jnp.exp(scores - top)
    return powers / jnp.sum(powers, axis=-1, keepdims=True)


def head_sum(value, ones):
    high = value.astype(jnp.bfloat16)
    rest = value - high.astype(jnp.float32)
    middle = rest.astype(jnp.bfloat16)
    small = (rest - middle.astype(jnp.float32)).astype(jnp.bfloat16)

    def part(piece):
        return jnp.dot(piece, ones, preferred_element_type=jnp.float32)

    return part(high) + (part(middle) + part(small))


def head_spread(value, ones):
    high = value.astype(jnp.bfloat16)
    rest = value - high.astype(jnp.float32)
    middle = rest.astype(jnp.bfloat16)
    small = (rest - middle.astype(jnp.float32)).astype(jnp.bfloat16)

    def part(piece):
        return lax.dot_general(
            piece, ones, (((1,), (1,)), ((), ())), preferred_element_type=jnp.float32
        )

    return part(high) + (part(middle) + part(small))


def temporal_probs(pair_ref, proj_ref, ones):
    width = HEADS * HEAD
    query = [proj_ref[r, :, 0:width] for r in range(FRAMES)]
    key = [proj_ref[r, :, width : 2 * width] for r in range(FRAMES)]
    both = pair_ref[0] > 0
    probs = []
    for r in range(FRAMES):
        scores = [head_sum(query[r] * key[s], ones) * HEAD ** (-0.5) for s in range(FRAMES)]
        scores = [
            scores[s] if s == r else jnp.where(both, scores[s], -1000000000.0)
            for s in range(FRAMES)
        ]
        top = scores[0]
        for s in range(1, FRAMES):
            top = jnp.maximum(top, scores[s])
        powers = [jnp.exp(score - top) for score in scores]
        total = powers[0]
        for s in range(1, FRAMES):
            total = total + powers[s]
        probs.append([power / total for power in powers])
    return query, key, probs


def temporal_forward_kernel(pair_ref, proj_ref, ones_ref, out_ref):
    width = HEADS * HEAD
    ones = ones_ref[...]
    _, _, probs = temporal_probs(pair_ref, proj_ref, ones)
    value = [proj_ref[s, :, 2 * width :] for s in range(FRAMES)]
    for r in range(FRAMES):
        mixed = head_spread(probs[r][0], ones) * value[0]
        for s in range(1, FRAMES):
            mixed = mixed + head_spread(probs[r][s], ones) * value[s]
        out_ref[r] = mixed.astype(out_ref.dtype)


def temporal_backward_kernel(pair_ref, proj_ref, grad_ref, ones_ref, out_ref):
    width = HEADS * HEAD
    ones = ones_ref[...]
    query, key, probs = temporal_probs(pair_ref, proj_ref, ones)
    value = [proj_ref[s, :, 2 * width :] for s in range(FRAMES)]
    grad = [grad_ref[r].astype(jnp.float32) for r in range(FRAMES)]
    slope = []
    for r in range(FRAMES):
        through = [head_sum(grad[r] * value[s], ones) for s in range(FRAMES)]
        inner = probs[r][0] * through[0]
        for s in range(1, FRAMES):
            inner = inner + probs[r][s] * through[s]
        slope.append(
            [
                head_spread(probs[r][s] * (through[s] - inner) * HEAD ** (-0.5), ones)
                for s in range(FRAMES)
            ]
        )
    for r in range(FRAMES):
        d_query = slope[r][0] * key[0]
        for s in range(1, FRAMES):
            d_query = d_query + slope[r][s] * key[s]
        out_ref[r, :, 0:width] = d_query.astype(out_ref.dtype)
    for s in range(FRAMES):
        d_key = slope[0][s] * query[0]
        d_value = head_spread(probs[0][s], ones) * grad[0]
        for r in range(1, FRAMES):
            d_key = d_key + slope[r][s] * query[r]
            d_value = d_value + head_spread(probs[r][s], ones) * grad[r]
        out_ref[s, :, width : 2 * width] = d_key.astype(out_ref.dtype)
        out_ref[s, :, 2 * width :] = d_value.astype(out_ref.dtype)


def head_ones():
    lane = jnp.arange(HEADS * HEAD, dtype=jnp.int32)[:, None] // HEAD
    return (lane == jnp.arange(128, dtype=jnp.int32)[None, :]).astype(jnp.bfloat16)


TEMPORAL_ROWS = 64


def temporal_call(kernel, pair, arrays, columns):
    rows = arrays[0].shape[1]
    step = min(TEMPORAL_ROWS, rows)
    ones = head_ones()
    return pl.pallas_call(
        kernel,
        grid=(rows // step,),
        in_specs=[pl.BlockSpec(memory_space=pltpu.SMEM)]
        + [
            pl.BlockSpec((FRAMES, step, array.shape[2]), lambda i: (0, i, 0)) for array in arrays
        ]
        + [pl.BlockSpec(ones.shape, lambda i: (0, 0))],
        out_specs=pl.BlockSpec((FRAMES, step, columns), lambda i: (0, i, 0)),
        out_shape=jax.ShapeDtypeStruct((FRAMES, rows, columns), jnp.bfloat16),
        compiler_params=pltpu.CompilerParams(vmem_limit_bytes=48 * 1024 * 1024),
        cost_estimate=pl.CostEstimate(
            flops=20 * FRAMES * rows * columns * 128, bytes_accessed=16000000, transcendentals=0
        ),
    )(pair, *arrays, ones)


def temporal_mix(projected, pair):
    width = HEADS * HEAD
    shaped = projected.reshape(FRAMES, -1, 3 * width)
    return temporal_call(temporal_forward_kernel, pair, (shaped,), width).reshape(-1, width)


def temporal_pull(projected, grad, pair):
    width = HEADS * HEAD
    shaped = projected.reshape(FRAMES, -1, 3 * width)
    grad = grad.reshape(FRAMES, -1, width)
    return temporal_call(temporal_backward_kernel, pair, (shaped, grad), 3 * width).reshape(
        -1, 3 * width
    )


def product(left, right):
    return jnp.dot(left, right, preferred_element_type=jnp.float32)


def transposed(left, right):
    return lax.dot_general(
        left, right, (((0,), (0,)), ((), ())), preferred_element_type=jnp.float32
    )


def against(left, right):
    return lax.dot_general(
        left, right, (((1,), (1,)), ((), ())), preferred_element_type=jnp.float32
    )


def gradient(left, right):
    return transposed(right, left).astype(jnp.bfloat16)


def column_sum(value):
    return jnp.sum(value, axis=0, dtype=jnp.float32)


def spatial_mask(kind, tokens):
    segment = jnp.where(kind == 0, jnp.arange(tokens) // PATCH, 0)
    return segment[:, None] == segment[None, :]


def frame_pairs(kind, count):
    return ((kind == 0) & (count == 2)).astype(jnp.int32).reshape(1)


def masked_scores(queries, keys, allowed):
    scores = jnp.einsum(
        "lhe,mhe->hlm", queries, keys, preferred_element_type=jnp.float32
    ) * HEAD ** (-0.5)
    return jnp.where(allowed[None], scores, -1000000000.0)


def attend_forward(queries, keys, values, allowed):
    scores = masked_scores(queries, keys, allowed)
    top = jnp.max(scores, axis=-1, keepdims=True)
    powers = jnp.exp(scores - top)
    total = jnp.sum(powers, axis=-1, keepdims=True)
    probs = (powers / total).astype(jnp.bfloat16)
    mixed = jnp.einsum("hlm,mhe->lhe", probs, values, preferred_element_type=jnp.float32)
    return (mixed, top + jnp.log(total))


def attend_backward(queries, keys, values, allowed, logsum, upstream):
    scale = HEAD ** (-0.5)
    probs = jnp.exp(masked_scores(queries, keys, allowed) - logsum)
    through = jnp.einsum("lhe,mhe->hlm", upstream, values, preferred_element_type=jnp.float32)
    inner = jnp.sum(probs * through, axis=-1, keepdims=True)
    slopes = (probs * (through - inner)).astype(jnp.bfloat16)
    d_queries = (
        jnp.einsum("hlm,mhe->lhe", slopes, keys, preferred_element_type=jnp.float32) * scale
    ).astype(jnp.bfloat16)
    d_keys = (
        jnp.einsum("hlm,lhe->mhe", slopes, queries, preferred_element_type=jnp.float32) * scale
    ).astype(jnp.bfloat16)
    d_values = jnp.einsum(
        "hlm,lhe->mhe", probs.astype(jnp.bfloat16), upstream, preferred_element_type=jnp.float32
    ).astype(jnp.bfloat16)
    return (d_queries, d_keys, d_values)


GROUPS = ((0, 1), (2, 3, 4, 5, 6), (7, 8))
BACK_GROUPS = ((8,), (7,), (4, 5, 6), (2, 3), (0, 1))


def to_rows(value, columns):
    flat = value.reshape(value.shape[:-1] + (-1,)) if value.ndim > 1 else value
    flat = value.reshape(-1)
    rows = -(-flat.shape[0] // (8 * columns)) * 8
    return jnp.pad(flat, (0, rows * columns - flat.shape[0])).reshape(rows, columns)


def as_rows(shard, columns):
    return shard.T.reshape(-1, columns)


def collect(shards):
    wide, narrow = lax.axis_size("wide"), lax.axis_size("narrow")
    columns = shards[0].shape[0]
    weights = [None] * 9
    for number, group in enumerate(GROUPS):
        pieces = [as_rows(shards[index], columns) for index in group]
        if number == 0:
            pieces += [to_rows(shards[9], columns), to_rows(shards[10], columns)]
        packed = jnp.concatenate(pieces, axis=0)
        whole = lax.all_gather(packed, ("wide", "narrow"), axis=0, tiled=True)
        whole = whole.reshape(wide, narrow, packed.shape[0], columns)
        start = 0
        for place, piece in enumerate(pieces):
            part = whole[:, :, start : start + piece.shape[0]]
            start += piece.shape[0]
            if place < len(group):
                index = group[place]
                own, depth = shards[index].shape[1], shards[index].shape[0]
                part = part.reshape(wide, narrow, own, depth // columns, columns)
                part = part.transpose(0, 2, 1, 3, 4)
                weights[index] = part.reshape(wide * own, narrow * depth)
            elif place == len(group):
                rows, own = shards[9].shape
                part = part.reshape(wide, narrow, -1)[:, :, : rows * own]
                part = part.reshape(wide, narrow, rows, own).transpose(1, 2, 0, 3)
                vectors = part.reshape(narrow * rows, wide * own)
            else:
                bias = part.reshape(wide * narrow, -1)[:, : shards[10].shape[0]].reshape(-1)
    return tuple(weights) + (vectors, bias)


def spread(grads, shards):
    wide, narrow = lax.axis_size("wide"), lax.axis_size("narrow")
    columns = shards[0].shape[0]
    result = [None] * 11
    for number, group in enumerate(BACK_GROUPS):
        pieces = []
        for index in group:
            depth, own = shards[index].shape
            part = grads[index].reshape(wide, own, narrow, depth // columns, columns)
            pieces.append(part.transpose(0, 2, 1, 3, 4).reshape(wide, narrow, -1, columns))
        if number == len(BACK_GROUPS) - 1:
            rows, own = shards[9].shape
            part = grads[9].astype(jnp.bfloat16).reshape(narrow, rows, wide, own)
            part = part.transpose(2, 0, 1, 3).reshape(wide * narrow, -1)
            pieces.append(jax.vmap(partial(to_rows, columns=columns))(part))
            part = grads[10].astype(jnp.bfloat16).reshape(wide * narrow, -1)
            pieces.append(jax.vmap(partial(to_rows, columns=columns))(part))
            pieces[-2:] = [
                piece.reshape(wide, narrow, -1, columns) for piece in pieces[-2:]
            ]
        packed = jnp.concatenate(pieces, axis=2)
        count = packed.shape[2]
        mine = lax.psum_scatter(
            packed.reshape(wide * narrow * count, columns),
            ("wide", "narrow"),
            scatter_dimension=0,
            tiled=True,
        ).astype(jnp.float32)
        start = 0
        for place, piece in enumerate(pieces):
            part = mine[start : start + piece.shape[2]]
            start += piece.shape[2]
            if place < len(group):
                depth, own = shards[group[place]].shape
                result[group[place]] = part.reshape(own, depth).T
            else:
                shard = shards[9 + place - len(group)]
                result[9 + place - len(group)] = part.reshape(-1)[: shard.size].reshape(
                    shard.shape
                )
    return tuple(result)


def clip_forward(weights, block, words, table_in, length, kind, count):
    (
        spatial_in,
        spatial_out,
        temporal_in,
        temporal_out,
        cross_query,
        cross_keyval,
        cross_out,
        feed_up,
        feed_down,
        vectors,
        feed_bias,
    ) = weights
    tokens = FRAMES * PATCH
    width = HEADS * HEAD
    rows = vectors.astype(jnp.float32)
    table = rows[0:6] + table_in
    blank = jnp.zeros((width,), jnp.float32)
    flat = block.reshape(tokens, width)
    entered = modulate(flat, table[0], table[1]).astype(jnp.bfloat16)
    packed = (
        (against(entered, spatial_in) + jnp.concatenate([rows[6], blank, rows[7]]))
        .astype(jnp.bfloat16)
        .reshape(tokens, 3, HEADS, HEAD)
    )
    mixed, spatial_sum = attend_forward(
        packed[:, 0], packed[:, 1], packed[:, 2], spatial_mask(kind, tokens)
    )
    attended = mixed.reshape(tokens, width).astype(jnp.bfloat16)
    spatial = against(attended, spatial_out) + rows[8]
    first = flat + table[2] * spatial
    temporal_proj = against(first.astype(jnp.bfloat16), temporal_in) + jnp.concatenate(
        [rows[9], blank, rows[10]]
    )
    temporal_att = temporal_mix(temporal_proj, frame_pairs(kind, count))
    temporal = against(temporal_att, temporal_out) + rows[11]
    second = first + table[2] * temporal
    query_text = (
        (against(second.astype(jnp.bfloat16), cross_query) + rows[12])
        .astype(jnp.bfloat16)
        .reshape(tokens, HEADS, HEAD)
    )
    keyval = (
        (against(words.astype(jnp.bfloat16), cross_keyval) + jnp.concatenate([blank, rows[13]]))
        .astype(jnp.bfloat16)
        .reshape(-1, 2, HEADS, HEAD)
    )
    text_mask = (jnp.arange(words.shape[0]) < length)[None, :]
    mixed, cross_sum = attend_forward(query_text, keyval[:, 0], keyval[:, 1], text_mask)
    cross_att = mixed.reshape(tokens, width).astype(jnp.bfloat16)
    third = second + (against(cross_att, cross_out) + rows[14])
    normed = modulate(third, table[3], table[4]).astype(jnp.bfloat16)
    hidden = against(normed, feed_up) + feed_bias.astype(jnp.float32)
    activated = jax.nn.gelu(hidden, approximate=True).astype(jnp.bfloat16)
    feed = against(activated, feed_down) + rows[15]
    result = third + table[5] * feed
    saved = (
        entered,
        packed,
        spatial_sum,
        attended,
        spatial,
        first,
        temporal_proj,
        temporal_att,
        temporal,
        second,
        query_text,
        keyval,
        cross_sum,
        cross_att,
        third,
        normed,
        hidden,
        activated,
        feed,
    )
    return (result.reshape(FRAMES, PATCH, width), saved)


def clip_backward(weights, saved, block, words, table_in, length, kind, count, upstream):
    (
        spatial_in,
        spatial_out,
        temporal_in,
        temporal_out,
        cross_query,
        cross_keyval,
        cross_out,
        feed_up,
        feed_down,
        vectors,
        feed_bias,
    ) = weights
    (
        entered,
        packed,
        spatial_sum,
        attended,
        spatial,
        first,
        temporal_proj,
        temporal_att,
        temporal,
        second,
        query_text,
        keyval,
        cross_sum,
        cross_att,
        third,
        normed,
        hidden,
        activated,
        feed,
    ) = saved
    tokens = FRAMES * PATCH
    width = HEADS * HEAD
    table = vectors.astype(jnp.float32)[0:6] + table_in
    flat = block.reshape(tokens, width)
    upstream = upstream.reshape(tokens, width)
    d_feed = (table[5] * upstream).astype(jnp.bfloat16)
    grad_down = gradient(activated, d_feed)
    gate_b = jnp.sum(upstream * feed, axis=0)
    _, gelu_pull = jax.vjp(partial(jax.nn.gelu, approximate=True), hidden)
    d_hidden = gelu_pull(product(d_feed, feed_down))[0].astype(jnp.bfloat16)
    grad_up = gradient(normed, d_hidden)
    _, norm_pull = jax.vjp(modulate, third, table[3], table[4])
    d_third, shift_b, scale_b = norm_pull(product(d_hidden, feed_up))
    d_third = upstream + d_third
    d_cross = d_third.astype(jnp.bfloat16)
    grad_cross_out = gradient(cross_att, d_cross)
    d_cross_att = product(d_cross, cross_out).astype(jnp.bfloat16).reshape(tokens, HEADS, HEAD)
    text_mask = (jnp.arange(words.shape[0]) < length)[None, :]
    d_query, d_key, d_value = attend_backward(
        query_text, keyval[:, 0], keyval[:, 1], text_mask, cross_sum, d_cross_att
    )
    d_query = d_query.reshape(tokens, width)
    d_keyval = jnp.concatenate([d_key.reshape(-1, width), d_value.reshape(-1, width)], axis=1)
    grad_query = gradient(second.astype(jnp.bfloat16), d_query)
    grad_keyval = gradient(words.astype(jnp.bfloat16), d_keyval)
    d_text = product(d_keyval, cross_keyval)
    d_second = d_third + product(d_query, cross_query)
    d_temporal = (table[2] * d_second).astype(jnp.bfloat16)
    gate_a = jnp.sum(d_second * temporal, axis=0)
    grad_temporal_out = gradient(temporal_att, d_temporal)
    d_mixed = product(d_temporal, temporal_out).astype(jnp.bfloat16)
    d_temporal_proj = temporal_pull(temporal_proj, d_mixed, frame_pairs(kind, count))
    grad_temporal_in = gradient(first.astype(jnp.bfloat16), d_temporal_proj)
    d_first = d_second + product(d_temporal_proj, temporal_in)
    d_spatial = (table[2] * d_first).astype(jnp.bfloat16)
    gate_a = gate_a + jnp.sum(d_first * spatial, axis=0)
    grad_spatial_out = gradient(attended, d_spatial)
    d_attended = product(d_spatial, spatial_out).astype(jnp.bfloat16).reshape(tokens, HEADS, HEAD)
    d_query_s, d_key_s, d_value_s = attend_backward(
        packed[:, 0],
        packed[:, 1],
        packed[:, 2],
        spatial_mask(kind, tokens),
        spatial_sum,
        d_attended,
    )
    d_packed = jnp.concatenate(
        [
            d_query_s.reshape(tokens, width),
            d_key_s.reshape(tokens, width),
            d_value_s.reshape(tokens, width),
        ],
        axis=1,
    )
    grad_spatial_in = gradient(entered, d_packed)
    _, input_pull = jax.vjp(modulate, flat, table[0], table[1])
    d_flat, shift_a, scale_a = input_pull(product(d_packed, spatial_in))
    d_input = d_first + d_flat
    packed_sum = column_sum(d_packed)
    temporal_sum = column_sum(d_temporal_proj)
    vector_grad = jnp.stack(
        [
            shift_a,
            scale_a,
            gate_a,
            shift_b,
            scale_b,
            gate_b,
            packed_sum[:width],
            packed_sum[2 * width :],
            column_sum(d_spatial),
            temporal_sum[:width],
            temporal_sum[2 * width :],
            column_sum(d_temporal),
            column_sum(d_query),
            column_sum(d_keyval)[width:],
            column_sum(d_cross),
            column_sum(d_feed),
        ]
    )
    terms = (
        grad_spatial_in,
        grad_spatial_out,
        grad_temporal_in,
        grad_temporal_out,
        grad_query,
        grad_keyval,
        grad_cross_out,
        grad_up,
        grad_down,
        vector_grad,
        column_sum(d_hidden),
    )
    return (terms, d_input.reshape(FRAMES, PATCH, width), d_text)


def local(
    block_input,
    text,
    modulation,
    text_lengths,
    bucket,
    frames,
    cotangent,
    spatialqkv,
    spatialout,
    temporalqkv,
    temporalout,
    crossquery,
    crosskeyval,
    crossout,
    feedup,
    feeddown,
    vectors,
    feedbias,
):
    low_shards = tuple(
        (
            piece.astype(jnp.bfloat16)
            for piece in (
                spatialqkv,
                spatialout,
                temporalqkv,
                temporalout,
                crossquery,
                crosskeyval,
                crossout,
                feedup,
                feeddown,
                vectors,
                feedbias,
            )
        )
    )
    weights = collect(low_shards)
    count = block_input.shape[0]
    outputs, input_grads, text_grads, totals = [], [], [], None
    for sample in range(count):
        items = (
            block_input[sample],
            text[sample],
            modulation[sample],
            text_lengths[sample],
            bucket[sample],
            frames[sample],
        )
        result, saved = clip_forward(weights, *items)
        terms, d_input, d_text = clip_backward(weights, saved, *items, cotangent[sample])
        outputs.append(result)
        input_grads.append(d_input)
        text_grads.append(d_text)
        if totals is None:
            totals = terms
        else:
            totals = tuple(
                (total.astype(jnp.float32) + term).astype(term.dtype)
                for total, term in zip(totals, terms)
            )
    return (jnp.stack(outputs), jnp.stack(input_grads), jnp.stack(text_grads)) + spread(
        totals, low_shards
    )


def solution(mesh):
    return jax.shard_map(
        local,
        mesh=mesh,
        in_specs=(
            P(("wide", "narrow"), None, None, None),
            P(("wide", "narrow"), None, None),
            P(("wide", "narrow"), None, None),
            P(("wide", "narrow")),
            P(("wide", "narrow")),
            P(("wide", "narrow")),
            P(("wide", "narrow"), None, None, None),
            P("narrow", "wide"),
            P("narrow", "wide"),
            P("narrow", "wide"),
            P("narrow", "wide"),
            P("narrow", "wide"),
            P("narrow", "wide"),
            P("narrow", "wide"),
            P("narrow", "wide"),
            P("narrow", "wide"),
            P("narrow", "wide"),
            P(("wide", "narrow")),
        ),
        out_specs=(
            P(("wide", "narrow"), None, None, None),
            P(("wide", "narrow"), None, None, None),
            P(("wide", "narrow"), None, None),
            P("narrow", "wide"),
            P("narrow", "wide"),
            P("narrow", "wide"),
            P("narrow", "wide"),
            P("narrow", "wide"),
            P("narrow", "wide"),
            P("narrow", "wide"),
            P("narrow", "wide"),
            P("narrow", "wide"),
            P("narrow", "wide"),
            P(("wide", "narrow")),
        ),
        check_vma=False,
    )
```
